32 devices in a mesh: island: 8 (over y, x, core), fsdp: 4 (over z).
Axes of the slice: x: 2, y: 2, z: 4, core: 2. Of those that a mesh axis runs over, the one named last changes fastest.
Arguments:
- tokens: bfloat16 [8, 1024, 8192], P('island', 'fsdp'), may hold values from -6 to 6
- cotangent: bfloat16 [8, 1024, 1024], P('island', 'fsdp'), may hold values from -0.1875 to 0.1875
- params: float32 [8, 8192, 1024], P('island', 'fsdp'), may hold values from -0.18 to 0.18
- first_moment: bfloat16 [8, 8192, 1024], P('island', 'fsdp'), may hold values from -3 to 3
- second_moment: bfloat16 [8, 8192, 1024], P('island', 'fsdp'), may hold values from 0.25 to 4
- base: float32 [8192, 512], P(('fsdp', 'island')), may hold values from -0.18 to 0.18
- outer_momentum: float32 [8192, 512], P(('fsdp', 'island')), may hold values from -0.06 to 0.06
- head_order: int32 [8], replicated, may hold values from 0 to 7, each once
- step_fragment: int32 [1], replicated, may hold values from 0 to 1
Outputs:
- params_out: float32 [8, 8192, 1024], P('island', 'fsdp')
- first_out: bfloat16 [8, 8192, 1024], P('island', 'fsdp')
- second_out: bfloat16 [8, 8192, 1024], P('island', 'fsdp')
- base_out: float32 [8192, 512], P(('fsdp', 'island'))
- momentum_out: float32 [8192, 512], P(('fsdp', 'island'))
The draws below stay inside these ranges and needn't reach their ends.
All inputs are finite; a program needn't handle non-finite values.
Results may differ from the reference program's by a relative error of at most 0.012.
Values may be sent and summed in bfloat16 or wider, within the bound.
No kernel may reach another device: no remote copies, remote signals or barrier semaphores. Data moves between devices by JAX's collectives and lax.ppermute only.
A program may use at most 128 MiB of HBM per device.

```python
import math
import jax
import jax.numpy as jnp
from jax import lax

D = 8192
KVH = 8
HD = 128
SYNC = 4
TOK_DEV = 256
KV = 1024
FC = 512
FRAGS = 2
TOKENS = 1024
N_ISLAND = 8
N_FSDP = 4


def with_spikes(drawn, rng, source, target, parts, factor):
    owner, partner = [(jnp.arange(drawn.shape[position]) // (drawn.shape[position] // parts)).reshape([-1 if axis == position else 1 for axis in range(drawn.ndim)]) for position in (source, target)]
    chosen = jax.random.permutation(rng, parts)[partner]
    strong = (owner == chosen) | (owner == (partner + parts // 2) % parts)
    return jnp.where(strong, factor * drawn, drawn)


def block_scale(own_key, extent, split, low, largest):
    gain, own = 1.0, jax.random.fold_in(own_key, 6)
    for dim, blocks in split:
        draws = jnp.exp(jax.random.uniform(jax.random.fold_in(own, dim), (blocks,), jnp.float32, low / len(split), largest / len(split)))
        gain = gain * jnp.repeat(draws, extent[dim] // blocks).reshape([-1 if axis == dim else 1 for axis in range(len(extent))])
    return gain


def centred(key, extent, spread, bound, cuts=(), kind=jnp.bfloat16):
    loudness = block_scale(key, extent, cuts, -0.22, 0.18) if cuts else 1.0
    entries = jax.random.normal(key, extent, jnp.float32) * spread * loudness
    return jnp.minimum(jnp.maximum(entries, -bound), bound).astype(kind)


def bell_draw_with(stream_key, shape, spread, limit, split, heavy, kind=jnp.bfloat16):
    entries = spread * jax.random.normal(stream_key, shape, jnp.float32)
    if split:
        entries = entries * block_scale(stream_key, shape, split, -0.22, 0.18)
    return jnp.clip(with_spikes(entries, jax.random.fold_in(stream_key, 3), *heavy), -limit, limit).astype(kind)


def setup_inputs(seed: int = 0) -> dict:
    arg_keys = jax.random.split(jax.random.key(seed), 10)
    return {
        "tokens": bell_draw_with(arg_keys[0], (N_ISLAND, TOKENS, D), 1.0, 6.0, ((0, 8), (1, 4)), (1, 2, 4, 2.0)),
        "cotangent": centred(arg_keys[1], (N_ISLAND, TOKENS, KV), (TOKENS ** -0.5), 0.1875, ((0, 8), (1, 4))),
        "params": centred(arg_keys[2], (N_ISLAND, D, KV), 0.03, 0.18, ((0, 8), (1, 4)), jnp.float32),
        "first_moment": centred(arg_keys[3], (N_ISLAND, D, KV), 0.5, 3.0, ((0, 8), (1, 4))),
        "second_moment": jnp.clip(jnp.exp(math.log(4.0) - 2.7725887 * jax.random.uniform(arg_keys[4], (N_ISLAND, D, KV), jnp.float32) ** block_scale(arg_keys[4], (N_ISLAND, D, KV), ((0, 8), (1, 4)), -0.2, 0.2)), 0.25, 4.0).astype(jnp.bfloat16),
        "base": centred(arg_keys[5], (D, FC), 0.03, 0.18, ((0, 32),), jnp.float32),
        "outer_momentum": centred(arg_keys[6], (D, FC), 0.01, 0.06, ((0, 32),), jnp.float32),
        "head_order": jax.random.permutation(arg_keys[7], KVH).astype(jnp.int32),
        "step_fragment": jax.random.randint(arg_keys[8], (1,), 0, FRAGS).astype(jnp.int32),
    }


def inner_step(tokens, cotangent, params, first_moment, second_moment):
    token_blocks = tokens.reshape(N_FSDP, TOK_DEV, D)
    grad_blocks = cotangent.reshape(N_FSDP, TOK_DEV, KV)

    def add_block(total, pair):
        xs, ds = pair
        part = jnp.dot(xs.T, ds, preferred_element_type=jnp.float32)
        part = lax.optimization_barrier(part.astype(jnp.bfloat16)).astype(jnp.float32)
        return (total + part, None)
    grad, _ = lax.scan(add_block, jnp.zeros((D, KV), jnp.float32), (token_blocks, grad_blocks))
    moment_one = 0.9 * first_moment.astype(jnp.float32) + 0.1 * grad
    moment_two = 0.95 * second_moment.astype(jnp.float32) + 0.05 * grad * grad
    stepped = params - 0.01 * (moment_one / (jnp.sqrt(moment_two) + 1e-08) + 0.1 * params)
    return (stepped, moment_one.astype(jnp.bfloat16), moment_two.astype(jnp.bfloat16))

def reference(tokens, cotangent, params, first_moment, second_moment, base, outer_momentum, head_order, step_fragment):
    stepped, first_out, second_out = lax.map(lambda group: inner_step(*group), (tokens, cotangent, params, first_moment, second_moment))
    heads = lax.dynamic_slice(head_order, (step_fragment[0] * SYNC,), (SYNC,))
    shaped = stepped.reshape(N_ISLAND, D, KVH, HD)
    fragment = jnp.take(shaped, heads, axis=2).reshape(N_ISLAND, D, FC)
    delta = base - lax.optimization_barrier(jnp.sum(fragment, axis=0)) / N_ISLAND
    momentum_out = 0.9 * outer_momentum + delta
    base_out = base - 0.7 * (delta + 0.9 * momentum_out)
    placed = jnp.broadcast_to(base_out.reshape(1, D, SYNC, HD), (N_ISLAND, D, SYNC, HD))
    params_out = shaped.at[:, :, heads, :].set(placed).reshape(N_ISLAND, D, KV)
    return (params_out, first_out, second_out, base_out, momentum_out)
```

```python
import functools
import jax
import jax.numpy as jnp
from jax import lax
from jax.experimental import pallas as pl
from jax.experimental.pallas import tpu as pltpu
from jax.sharding import PartitionSpec as P

KVH = 8
HD = 128
SYNC = 4


def outer_update(base, outer_momentum, total, islands):
    delta = base - total / islands
    momentum = 0.9 * outer_momentum + delta
    return (base - 0.7 * (delta + 0.9 * momentum), momentum)


def vmem():
    return pl.BlockSpec(memory_space=pltpu.VMEM)


def cost(flops, moved):
    return pl.CostEstimate(flops=flops, bytes_accessed=moved, transcendentals=0)


def order_columns(order, cot, groups):
    rows = cot.shape[0]

    def kernel(order_ref, cot_ref, *out_refs):
        place = 0
        for group, out in zip(groups, out_refs):
            for j in range(group):
                start = pl.multiple_of(order_ref[place] * HD, HD)
                out[:, j * HD : (j + 1) * HD] = cot_ref[:, pl.ds(start, HD)]
                place += 1

    return pl.pallas_call(
        kernel,
        grid_spec=pltpu.PrefetchScalarGridSpec(
            num_scalar_prefetch=1,
            grid=(1,),
            in_specs=[pl.BlockSpec(cot.shape, lambda i, o: (0, 0))],
            out_specs=[pl.BlockSpec((rows, g * HD), lambda i, o: (0, 0)) for g in groups],
        ),
        out_shape=[jax.ShapeDtypeStruct((rows, g * HD), cot.dtype) for g in groups],
        cost_estimate=cost(0, 4 * cot.size),
        name="order_columns",
    )(order, cot)


def turn_tokens(dests, tokens, owners, span, lanes, cuts):
    depth = tokens.shape[0]
    first, count = lanes
    peers = dests.shape[0]

    def kernel(dest_ref, tok_ref, *out_refs):
        step = pl.program_id(0)
        turned = tok_ref[...].T
        for peer in range(peers):

            @pl.when(step == peer)
            def _():
                for c, (start, width) in enumerate(cuts):
                    out_refs[c * peers + peer][0] = turned[start - first : start - first + width]

    def place(peer):
        def index(s, i, d):
            return (jnp.where(s == peer, i, jnp.where(s < peer, 0, owners - 1)), 0, 0)

        return index

    outs = [(width, peer) for _, width in cuts for peer in range(peers)]
    per = span // count
    flat = pl.pallas_call(
        kernel,
        grid_spec=pltpu.PrefetchScalarGridSpec(
            num_scalar_prefetch=1,
            grid=(peers, owners),
            in_specs=[
                pl.BlockSpec(
                    (depth, count),
                    lambda s, i, d: (0, (d[s] * owners + i) * per + first // count),
                )
            ],
            out_specs=[pl.BlockSpec((1, w, depth), place(peer)) for w, peer in outs],
        ),
        out_shape=[jax.ShapeDtypeStruct((owners, w, depth), tokens.dtype) for w, _ in outs],
        cost_estimate=cost(0, 4 * peers * owners * count * depth),
        name="turn_tokens",
    )(dests, tokens)
    return [flat[c * peers : (c + 1) * peers] for c in range(len(cuts))]


def inner_step(order, spots, toks, cots, params, first, second, olds, place, k0, share):
    owners, span, _ = params.shape
    w, depth = toks[0].shape[1:]
    peers = len(toks)
    p0, heads = place
    wide = 2 if heads % 2 == 0 else 1
    rows = owners * w
    kb = k0 // w

    def kernel(order_ref, spot_ref, *refs):
        tok_refs = refs[:peers]
        cot_refs = refs[peers : 2 * peers]
        p_ref, m_ref, v_ref = refs[2 * peers : 2 * peers + 3]
        rest = refs[2 * peers + 3 :]
        if olds is not None:
            rest = rest[3:]
        po_ref, mo_ref, vo_ref = rest[:3]
        if share:
            keep_ref, send_ref = rest[3:5]
            grad_ref, frag_ref = rest[5:]
        else:
            (grad_ref,) = rest[3:]
        step = pl.program_id(0)

        @pl.when(lax.rem(step, wide) == 0)
        def _():
            left = jnp.concatenate([t[...].reshape(rows, depth) for t in tok_refs], axis=1)
            right = jnp.concatenate([c[...] for c in cot_refs], axis=0)
            product = jnp.dot(left, right, preferred_element_type=jnp.float32)
            for j in range(wide):
                grad_ref[j] = product[:, j * HD : (j + 1) * HD].reshape(owners, w, HD)

        grad = grad_ref[lax.rem(step, wide)]
        one = 0.9 * m_ref[...].astype(jnp.float32) + 0.1 * grad
        two = 0.95 * v_ref[...].astype(jnp.float32) + 0.05 * grad * grad
        old = p_ref[...]
        new = old - 0.01 * (one / (jnp.sqrt(two) + 1e-08) + 0.1 * old)
        mo_ref[...] = one.astype(mo_ref.dtype)
        vo_ref[...] = two.astype(vo_ref.dtype)
        po_ref[...] = new
        if share:
            frag_ref[...] = new.astype(frag_ref.dtype)
            for e in range(owners):
                piece = frag_ref[spot_ref[e]]
                (send_ref if e % 2 else keep_ref)[e // 2] = piece

    block = pl.BlockSpec((owners, w, HD), lambda p, o, s: (0, kb, o[p0 + p]))
    whole = pl.BlockSpec((owners, w, depth), lambda p, o, s: (0, 0, 0))
    column = pl.BlockSpec((depth, wide * HD), lambda p, o, s: (0, p // wide))
    half = pl.BlockSpec((owners // 2, w, HD), lambda p, o, s: (0, 0, p))
    in_specs = [whole] * peers + [column] * peers + [block] * 3
    args = [order, spots, *toks, *cots, params, first, second]
    aliases = {}
    if olds is not None:
        for i in range(3):
            aliases[len(args) + i] = i
        in_specs += [pl.BlockSpec(memory_space=pl.ANY)] * 3
        args += list(olds)
    out_shape = [
        jax.ShapeDtypeStruct(params.shape, params.dtype),
        jax.ShapeDtypeStruct(first.shape, first.dtype),
        jax.ShapeDtypeStruct(second.shape, second.dtype),
    ]
    out_specs = [block] * 3
    scratch = [pltpu.VMEM((wide, owners, w, HD), jnp.float32)]
    if share:
        out_shape += [jax.ShapeDtypeStruct((owners // 2, w, heads * HD), jnp.bfloat16)] * 2
        out_specs += [half] * 2
        scratch += [pltpu.VMEM((owners, w, HD), jnp.bfloat16)]
    outs = pl.pallas_call(
        kernel,
        grid_spec=pltpu.PrefetchScalarGridSpec(
            num_scalar_prefetch=2,
            grid=(heads,),
            in_specs=in_specs,
            out_specs=out_specs,
            scratch_shapes=scratch,
        ),
        out_shape=out_shape,
        input_output_aliases=aliases,
        cost_estimate=cost(
            2 * rows * depth * peers * heads * HD,
            rows * heads * HD * 16 + 2 * rows * depth * peers,
        ),
        name="inner_step",
    )(*args)
    return outs[:3], outs[3:]


def place_base(order, spots, near, far, params, k0):
    owners = params.shape[0]
    half, w, width = near.shape
    heads = width // HD

    def kernel(order_ref, spot_ref, near_ref, far_ref, old_ref, out_ref, stage, sems):
        for e in range(owners):
            source = (far_ref if e % 2 else near_ref)[e // 2].astype(jnp.float32)
            for j in range(heads):
                stage[j, spot_ref[e]] = source[:, j * HD : (j + 1) * HD]
        copies = []
        for j in range(heads):
            column = pl.multiple_of(order_ref[j] * HD, HD)
            target = out_ref.at[:, pl.ds(k0, w), pl.ds(column, HD)]
            copies.append(pltpu.make_async_copy(stage.at[j], target, sems.at[j]))
            copies[-1].start()
        for copy in copies:
            copy.wait()

    return pl.pallas_call(
        kernel,
        grid_spec=pltpu.PrefetchScalarGridSpec(
            num_scalar_prefetch=2,
            grid=(1,),
            in_specs=[
                pl.BlockSpec(near.shape, lambda i, o, s: (0, 0, 0)),
                pl.BlockSpec(far.shape, lambda i, o, s: (0, 0, 0)),
                pl.BlockSpec(memory_space=pl.ANY),
            ],
            out_specs=pl.BlockSpec(memory_space=pl.ANY),
            scratch_shapes=[
                pltpu.VMEM((heads, owners, w, HD), jnp.float32),
                pltpu.SemaphoreType.DMA((heads,)),
            ],
        ),
        out_shape=jax.ShapeDtypeStruct(params.shape, params.dtype),
        input_output_aliases={4: 0},
        cost_estimate=cost(0, owners * w * width * 8),
        name="place_base",
    )(order, spots, near, far, params)


def swap(x, axis, mask):
    size = lax.axis_size(axis)
    return lax.ppermute(x, axis, [(i, i ^ mask) for i in range(size)])


def line_gather(own):
    me = lax.axis_index("fsdp")
    near = swap(own, "fsdp", 1)
    pair = jnp.stack([own, near])
    across = lax.ppermute(pair, "fsdp", [(1, 2), (2, 1)])
    relay = lax.ppermute(across, "fsdp", [(1, 0), (2, 3)])
    inner = (me == 1) | (me == 2)
    return (
        near,
        jnp.where(inner, across[1], relay[0]),
        jnp.where(inner, across[0], relay[1]),
    )


def chunk_plan(span):
    return [(0, span // 2), (span // 2, span // 4), (3 * span // 4, span // 4)]


def staged(
    tokens,
    cotangent,
    params,
    first_moment,
    second_moment,
    base,
    outer_momentum,
    head_order,
    step_fragment,
):
    islands = lax.axis_size("island")
    peers = lax.axis_size("fsdp")
    rows, width = params.shape[1:]
    span = rows // islands
    me = lax.axis_index("fsdp").astype(jnp.int32)
    isle = lax.axis_index("island").astype(jnp.int32)
    turn = jnp.arange(KVH, dtype=jnp.int32) + step_fragment[0] * SYNC
    order = jnp.take(head_order, lax.rem(turn, KVH), axis=0)
    spots = jnp.arange(islands, dtype=jnp.int32) ^ isle
    dests = jnp.arange(peers, dtype=jnp.int32) ^ me

    (cot,) = order_columns(order, cotangent[0], (KVH,))
    near = line_gather(cot)
    cots = (cot, *near)

    plan = chunk_plan(span)
    half = span // 2
    turned = turn_tokens(dests, tokens[0], islands, span, (0, half), plan[:1])
    turned += turn_tokens(dests, tokens[0], islands, span, (half, half), plan[1:])

    shaped = [a[0].reshape(islands, span, width) for a in (params, first_moment, second_moment)]
    state = None
    bases, momenta = [], []
    pending = []
    for (k0, w), pieces in zip(plan, turned):
        toks = [pieces[0]] + [swap(pieces[e], "fsdp", e) for e in range(1, peers)]
        state, (keep, send) = inner_step(
            order, spots, toks, [c[:, : SYNC * HD] for c in cots], *shaped, state, (0, SYNC), k0, True
        )
        state, _ = inner_step(
            order, spots, toks, [c[:, SYNC * HD :] for c in cots], *shaped, state, (SYNC, KVH - SYNC), k0, False
        )
        got = swap(send, "island", 1)
        mask = 2
        part = keep.astype(jnp.float32) + got.astype(jnp.float32)
        while mask < islands:
            part = part.reshape(part.shape[0] // 2, 2, w, SYNC * HD)
            got = swap(part[:, 1].astype(jnp.bfloat16), "island", mask)
            part = part[:, 0] + got.astype(jnp.float32)
            mask *= 2
        new, mom = outer_update(
            base[k0 : k0 + w], outer_momentum[k0 : k0 + w], part[0], islands
        )
        bases.append(new)
        momenta.append(mom)
        spread = new.astype(jnp.bfloat16)[None]
        mask = islands // 2
        while mask > 1:
            got = swap(spread, "island", mask)
            spread = jnp.stack([spread, got], axis=1).reshape(-1, w, SYNC * HD)
            mask //= 2
        pending.append((k0, spread, swap(spread, "island", 1)))
    out = state[0]
    for k0, mine, other in pending:
        out = place_base(order, spots, mine, other, out, k0)
    return (
        out.reshape(1, rows, width),
        state[1].reshape(1, rows, width),
        state[2].reshape(1, rows, width),
        jnp.concatenate(bases),
        jnp.concatenate(momenta),
    )


def plain(
    tokens,
    cotangent,
    params,
    first_moment,
    second_moment,
    base,
    outer_momentum,
    head_order,
    step_fragment,
):
    local_tokens = tokens[0]
    weights = params[0]
    rows = weights.shape[0]
    width = weights.shape[1]
    block = local_tokens.shape[0]
    columns = lax.all_to_all(tokens, "fsdp", split_axis=2, concat_axis=1, tiled=True)[0]
    piece = lax.all_gather(cotangent, "fsdp", axis=1, tiled=True)
    blocks = piece.shape[1] // block

    def one_block(index, running):
        grads_part = lax.dynamic_slice_in_dim(piece[0], index * block, block, 0)
        token_part = lax.dynamic_slice_in_dim(columns, index * block, block, 0)
        part = lax.dot_general(
            token_part, grads_part, (((0,), (0,)), ((), ())), preferred_element_type=jnp.float32
        )
        part = lax.optimization_barrier(part.astype(jnp.bfloat16)).astype(jnp.float32)
        return running + part

    grad = lax.fori_loop(0, blocks, one_block, jnp.zeros((rows, width), jnp.float32))
    moment_one = 0.9 * first_moment[0].astype(jnp.float32) + 0.1 * grad
    moment_two = 0.95 * second_moment[0].astype(jnp.float32) + 0.05 * grad * grad
    stepped = weights - 0.01 * (moment_one / (jnp.sqrt(moment_two) + 1e-08) + 0.1 * weights)
    heads = lax.dynamic_slice(head_order, (step_fragment[0] * SYNC,), (SYNC,))
    shaped = stepped.reshape(rows, KVH, HD)
    fragment = jnp.take(shaped, heads, axis=1).reshape(rows, SYNC * HD)
    islands = lax.axis_size("island")
    total = lax.psum_scatter(
        fragment.astype(jnp.bfloat16), "island", scatter_dimension=0, tiled=True
    ).astype(jnp.float32)
    base_next, momentum_next = outer_update(base, outer_momentum, total, islands)
    whole_base = lax.all_gather(
        base_next.astype(jnp.bfloat16), "island", axis=0, tiled=True
    ).astype(base_next.dtype)
    updated = shaped.at[:, heads, :].set(whole_base.reshape(rows, SYNC, HD)).reshape(rows, width)
    return (
        updated[None],
        moment_one.astype(jnp.bfloat16)[None],
        moment_two.astype(jnp.bfloat16)[None],
        base_next,
        momentum_next,
    )


def shards(tokens, cotangent, params, *rest):
    islands = lax.axis_size("island")
    span = params.shape[1] // islands
    fits = lax.axis_size("fsdp") == 4 and islands >= 4 and islands & (islands - 1) == 0
    fits = fits and span % 256 == 0 and tokens.shape[1] % 128 == 0
    return (staged if fits else plain)(tokens, cotangent, params, *rest)


def solution(mesh):
    placed = (
        P("island", "fsdp", None),
        P("island", "fsdp", None),
        P("island", "fsdp", None),
        P("island", "fsdp", None),
        P("island", "fsdp", None),
        P(("fsdp", "island"), None),
        P(("fsdp", "island"), None),
        P(),
        P(),
    )
    return jax.shard_map(
        shards,
        mesh=mesh,
        in_specs=placed,
        out_specs=(
            P("island", "fsdp", None),
            P("island", "fsdp", None),
            P("island", "fsdp", None),
            P(("fsdp", "island"), None),
            P(("fsdp", "island"), None),
        ),
        check_vma=False,
    )
```

```python
import functools

import jax
import jax.numpy as jnp
from jax import lax
from jax.experimental import pallas as pl
from jax.experimental.pallas import tpu as pltpu
from jax.sharding import PartitionSpec as P


KVH = 8
HD = 128
SYNC = 4


def outer_update(base, outer_momentum, total, islands):
    delta = base - total / islands
    momentum = 0.9 * outer_momentum + delta
    return (base - 0.7 * (delta + 0.9 * momentum), momentum)


ANY = pl.BlockSpec(memory_space=pl.ANY)
HBM = pl.BlockSpec(memory_space=pltpu.HBM)


def cost(flops, moved):
    return pl.CostEstimate(flops=flops, bytes_accessed=moved, transcendentals=0)


def head_at(heads_ref, step_ref, position):
    return heads_ref[lax.rem(step_ref[0] * SYNC + position, KVH)]


def column(heads_ref, step_ref, position):
    return pl.ds(pl.multiple_of(head_at(heads_ref, step_ref, position) * HD, HD), HD)


VMEM_GRANT = 67043328 - 56 * 2**18


def call(
    kernel, scalars, args, outs, scratch, estimate, in_specs=None, out_specs=None, aliases=None
):
    return pl.pallas_call(
        kernel,
        grid_spec=pltpu.PrefetchScalarGridSpec(
            num_scalar_prefetch=len(scalars),
            grid=(1,),
            in_specs=in_specs or [ANY] * len(args),
            out_specs=out_specs or [ANY] * len(outs),
            scratch_shapes=scratch,
        ),
        out_shape=outs,
        input_output_aliases=aliases or {},
        cost_estimate=estimate,
        compiler_params=pltpu.CompilerParams(vmem_limit_bytes=VMEM_GRANT),
    )(*scalars, *args)


def turn_tokens(table, tokens, owners, peers, span, lanes, cuts):
    depth = tokens.shape[0]
    first, count = lanes

    def kernel(table_ref, tok_ref, *refs):
        outs = refs[: len(cuts) * peers]
        raw, in_sems, out_sems = refs[len(cuts) * peers : len(cuts) * peers + 3]
        stages = refs[len(cuts) * peers + 3 :]
        sequence = [*range(1, peers), 0]

        def load(e, i):
            start = (table_ref[owners + e] * owners + i) * span + first
            return pltpu.make_async_copy(
                tok_ref.at[:, pl.ds(pl.multiple_of(start, HD), count)],
                raw.at[e, i],
                in_sems.at[e, i],
            )

        for e in sequence:
            for i in range(owners):
                load(e, i).start()
        stores = []
        for e in sequence:
            for i in range(owners):
                load(e, i).wait()
                turned = raw[e, i].T
                for c, (start, width) in enumerate(cuts):
                    stages[c][e, i] = turned[start - first : start - first + width]
            for c in range(len(cuts)):
                stores.append(
                    pltpu.make_async_copy(
                        stages[c].at[e], outs[c * peers + e], out_sems.at[c, e]
                    )
                )
                stores[-1].start()
        for store in stores:
            store.wait()

    flat = call(
        kernel,
        (table,),
        (tokens,),
        [
            jax.ShapeDtypeStruct((owners, w, depth), tokens.dtype)
            for _, w in cuts
            for _ in range(peers)
        ],
        [
            pltpu.VMEM((peers, owners, depth, count), tokens.dtype),
            pltpu.SemaphoreType.DMA((peers, owners)),
            pltpu.SemaphoreType.DMA((len(cuts), peers)),
            *[pltpu.VMEM((peers, owners, w, depth), tokens.dtype) for _, w in cuts],
        ],
        cost(0, 4 * peers * owners * count * depth),
        in_specs=[HBM],
    )
    return [flat[c * peers : (c + 1) * peers] for c in range(len(cuts))]


def inner_step(heads, step, table, toks, cots, state, olds, place, k0):
    owners, _, _ = state[0].shape
    w, depth = toks[0].shape[1:]
    peers = len(toks)
    p0, count = place
    rows = owners * w
    shared = max(0, min(SYNC - p0, count))

    def kernel(heads_ref, step_ref, table_ref, *refs):
        tok_refs, refs = refs[:peers], refs[peers:]
        cot_refs, refs = refs[: len(cots)], refs[len(cots) :]
        sources, refs = refs[:3], refs[3:]
        if olds is not None:
            refs = refs[3:]
        targets, refs = refs[:3], refs[3:]
        if shared:
            keep_ref, send_ref, *refs = refs
        left, right, grad, p_s, m_s, v_s, tok_sems, cot_sems, in_sems, out_sems = refs
        parts = (p_s, m_s, v_s)
        me = table_ref[owners]
        isle = table_ref[0]
        inner = (me > 0) & (me < peers - 1)

        def tok_copy(e):
            return pltpu.make_async_copy(
                tok_refs[e], left.at[:, :, pl.ds(e * depth, depth)], tok_sems.at[e]
            )

        def cot_copy(e, k, j):
            return pltpu.make_async_copy(
                cot_refs[k].at[:, column(heads_ref, step_ref, p0 + j)],
                right.at[pl.ds(e * depth, depth), pl.ds(j * HD, HD)],
                cot_sems.at[e, j],
            )

        def window(ref, j):
            return ref.at[:, pl.ds(k0, w), column(heads_ref, step_ref, p0 + j)]

        def in_copy(n, j):
            return pltpu.make_async_copy(window(sources[n], j), parts[n].at[j], in_sems.at[n, j])

        def out_copy(n, j):
            return pltpu.make_async_copy(parts[n].at[j], window(targets[n], j), out_sems.at[n, j])

        for e in range(peers):
            tok_copy(e).start()
        for j in range(count):
            for e in range(2):
                cot_copy(e, e, j).start()
        for e in range(2, peers):

            @pl.when(inner)
            def _():
                for j in range(count):
                    cot_copy(e, 2 * e - 2, j).start()

            @pl.when(jnp.logical_not(inner))
            def _():
                for j in range(count):
                    cot_copy(e, 2 * e - 1, j).start()

        for j in range(count):
            for n in range(3):
                in_copy(n, j).start()
        for e in range(peers):
            tok_copy(e).wait()
            for j in range(count):
                cot_copy(e, e, j).wait()

        def update(j, lane, owner, target, slot):
            g = grad[owner, :, lane * HD : (lane + 1) * HD]
            one = 0.9 * m_s[j, owner].astype(jnp.float32) + 0.1 * g
            two = 0.95 * v_s[j, owner].astype(jnp.float32) + 0.05 * g * g
            old = p_s[j, owner]
            new = old - 0.01 * (one / (jnp.sqrt(two) + 1e-08) + 0.1 * old)
            m_s[j, owner] = one.astype(m_s.dtype)
            v_s[j, owner] = two.astype(v_s.dtype)
            p_s[j, owner] = new
            if target is not None:
                lanes = pl.ds(pl.multiple_of(j * HD, HD), HD)
                target[slot, :, lanes] = new.astype(target.dtype)

        def one_pair(share, pair, carry):
            lanes = pl.ds(pl.multiple_of(pair * 2 * HD, 2 * HD), 2 * HD)
            grad[...] = jnp.dot(
                left[...].reshape(rows, peers * depth),
                right[:, lanes],
                preferred_element_type=jnp.float32,
            ).reshape(owners, w, 2 * HD)
            for lane in range(2):
                j = 2 * pair + lane
                for n in range(3):
                    in_copy(n, j).wait()

                def two_owners(slot, carry):
                    for odd, target in enumerate((keep_ref, send_ref) if share else (None, None)):
                        update(j, lane, (2 * slot + odd) ^ isle, target, slot)
                    return carry

                lax.fori_loop(0, owners // 2, two_owners, 0)
                for n in range(3):
                    out_copy(n, j).start()
            return carry

        if shared:
            lax.fori_loop(0, shared // 2, functools.partial(one_pair, True), 0)
        if shared < count:
            lax.fori_loop(shared // 2, count // 2, functools.partial(one_pair, False), 0)
        for j in range(count):
            for n in range(3):
                out_copy(n, j).wait()

    args = [*toks, *cots, *state]
    aliases = {}
    if olds is not None:
        for i in range(3):
            aliases[3 + len(args) + i] = i
        args += list(olds)
    outs = [jax.ShapeDtypeStruct(a.shape, a.dtype) for a in state]
    out_specs = [HBM] * 3
    if shared:
        piece = (owners // 2, w, shared * HD)
        outs += [jax.ShapeDtypeStruct(piece, jnp.bfloat16)] * 2
        out_specs += [pl.BlockSpec(piece, lambda i, *_: (0, 0, 0))] * 2
    states = [HBM] * (6 if olds is not None else 3)
    result = call(
        kernel,
        (heads, step, table),
        args,
        outs,
        [
            pltpu.VMEM((owners, w, peers * depth), toks[0].dtype),
            pltpu.VMEM((peers * depth, count * HD), cots[0].dtype),
            pltpu.VMEM((owners, w, 2 * HD), jnp.float32),
            *[pltpu.VMEM((count, owners, w, HD), a.dtype) for a in state],
            pltpu.SemaphoreType.DMA((peers,)),
            pltpu.SemaphoreType.DMA((peers, count)),
            pltpu.SemaphoreType.DMA((3, count)),
            pltpu.SemaphoreType.DMA((3, count)),
        ],
        cost(
            2 * rows * depth * peers * count * HD,
            rows * count * HD * 16 + 2 * rows * depth * peers,
        ),
        in_specs=[ANY] * (len(toks) + len(cots)) + states,
        out_specs=out_specs,
        aliases=aliases,
    )
    return result[:3], result[3:]


def place_base(heads, step, table, news, params, starts):
    owners = params.shape[0]
    shapes = [near.shape for near, _ in news]
    count = shapes[0][2] // HD

    def kernel(heads_ref, step_ref, table_ref, *refs):
        pieces, refs = refs[: 2 * len(news)], refs[2 * len(news) + 1 :]
        out_ref, stages, sems = refs[0], refs[1:-1], refs[-1]
        isle = table_ref[0]
        copies = []
        for c, (k0, shape) in enumerate(zip(starts, shapes)):
            for j in range(count):
                for e in range(owners):
                    source = pieces[2 * c + e % 2][e // 2, :, j * HD : (j + 1) * HD]
                    stages[c][j, e ^ isle] = source.astype(jnp.float32)
                target = out_ref.at[:, pl.ds(k0, shape[1]), column(heads_ref, step_ref, j)]
                copies.append(pltpu.make_async_copy(stages[c].at[j], target, sems.at[c, j]))
                copies[-1].start()
        for copy in copies:
            copy.wait()

    (out,) = call(
        kernel,
        (heads, step, table),
        (*[x for pair in news for x in pair], params),
        [jax.ShapeDtypeStruct(params.shape, params.dtype)],
        [
            *[pltpu.VMEM((count, owners, shape[1], HD), jnp.float32) for shape in shapes],
            pltpu.SemaphoreType.DMA((len(news), count)),
        ],
        cost(0, sum(owners * shape[1] * shape[2] * 8 for shape in shapes)),
        in_specs=[
            pl.BlockSpec(shape, lambda i, *_: (0, 0, 0)) for shape in shapes for _ in range(2)
        ]
        + [HBM],
        out_specs=[HBM],
        aliases={3 + 2 * len(news): 0},
    )
    return out


def swap(x, axis, mask):
    return lax.ppermute(x, axis, [(i, i ^ mask) for i in range(lax.axis_size(axis))])


def line_gather(own):
    middle, ends = [(1, 2), (2, 1)], [(1, 0), (2, 3)]
    near = swap(own, "fsdp", 1)
    far = lax.ppermute(own, "fsdp", middle)
    next_far = lax.ppermute(near, "fsdp", middle)
    relay = lax.ppermute(far, "fsdp", ends)
    next_relay = lax.ppermute(next_far, "fsdp", ends)
    return [own, near, next_far, relay, far, next_relay]


def island_sum(keep, give):
    got = swap(give, "island", 1)
    part = keep.astype(jnp.float32) + got.astype(jnp.float32)
    total = part[0]
    for d in range(1, part.shape[0]):
        piece = part[d].astype(jnp.bfloat16)
        total = total + swap(piece, "island", 2 * d).astype(jnp.float32)
    return total


def island_spread(own):
    chips = lax.axis_size("island") // 2
    pieces = [own] + [swap(own, "island", 2 * d) for d in range(1, chips)]
    near = jnp.stack(pieces)
    return near, swap(near, "island", 1)


PLAN = ((0, 9), (9, 4), (13, 3))
PARTS = 16


def staged(
    tokens,
    cotangent,
    params,
    first_moment,
    second_moment,
    base,
    outer_momentum,
    head_order,
    step_fragment,
):
    islands = lax.axis_size("island")
    peers = lax.axis_size("fsdp")
    rows, width = params.shape[1:]
    span = rows // islands
    me = lax.axis_index("fsdp").astype(jnp.int32)
    isle = lax.axis_index("island").astype(jnp.int32)
    slots = jnp.arange(islands + peers, dtype=jnp.int32)
    table = jnp.where(slots < islands, slots ^ isle, (slots - islands) ^ me)
    hs = (head_order, step_fragment)

    cots = line_gather(cotangent[0])
    plan = [(k * span // PARTS, n * span // PARTS) for k, n in PLAN]
    last = len(plan) - 1
    edge = -(-plan[0][1] // HD) * HD
    turned = turn_tokens(table, tokens[0], islands, peers, span, (0, edge), plan[:1])
    edge = plan[1][0] // HD * HD
    turned += turn_tokens(
        table, tokens[0], islands, peers, span, (edge, span - edge), plan[1:]
    )
    toks = [
        [pieces[0]] + [swap(pieces[e], "fsdp", e) for e in range(1, peers)]
        for pieces in turned
    ]

    state = [a[0].reshape(islands, span, width) for a in (params, first_moment, second_moment)]
    olds = None
    bases, momenta, news = [], [], []

    def run(c, place):
        return inner_step(*hs, table, toks[c], cots, state, olds, place, plan[c][0])

    for c, (k0, w) in enumerate(plan):
        if c < last:
            olds, pieces = run(c, (0, KVH))
        else:
            olds, pieces = run(c, (0, SYNC))
            olds, _ = run(c, (SYNC, KVH - SYNC))
        total = island_sum(*pieces)
        new, mom = outer_update(base[k0 : k0 + w], outer_momentum[k0 : k0 + w], total, islands)
        bases.append(new)
        momenta.append(mom)
        news.append(island_spread(new.astype(jnp.bfloat16)))
    starts = [k0 for k0, _ in plan]
    out = place_base(*hs, table, news[:last], olds[0], starts[:last])
    out = place_base(*hs, table, news[last:], out, starts[last:])
    return (
        out.reshape(1, rows, width),
        olds[1].reshape(1, rows, width),
        olds[2].reshape(1, rows, width),
        jnp.concatenate(bases),
        jnp.concatenate(momenta),
    )


def plain(
    tokens,
    cotangent,
    params,
    first_moment,
    second_moment,
    base,
    outer_momentum,
    head_order,
    step_fragment,
):
    local_tokens = tokens[0]
    weights = params[0]
    rows = weights.shape[0]
    width = weights.shape[1]
    block = local_tokens.shape[0]
    columns = lax.all_to_all(tokens, "fsdp", split_axis=2, concat_axis=1, tiled=True)[0]
    piece = lax.all_gather(cotangent, "fsdp", axis=1, tiled=True)
    blocks = piece.shape[1] // block

    def one_block(index, running):
        grads_part = lax.dynamic_slice_in_dim(piece[0], index * block, block, 0)
        token_part = lax.dynamic_slice_in_dim(columns, index * block, block, 0)
        part = lax.dot_general(
            token_part, grads_part, (((0,), (0,)), ((), ())), preferred_element_type=jnp.float32
        )
        part = lax.optimization_barrier(part.astype(jnp.bfloat16)).astype(jnp.float32)
        return running + part

    grad = lax.fori_loop(0, blocks, one_block, jnp.zeros((rows, width), jnp.float32))
    moment_one = 0.9 * first_moment[0].astype(jnp.float32) + 0.1 * grad
    moment_two = 0.95 * second_moment[0].astype(jnp.float32) + 0.05 * grad * grad
    stepped = weights - 0.01 * (moment_one / (jnp.sqrt(moment_two) + 1e-08) + 0.1 * weights)
    heads = lax.dynamic_slice(head_order, (step_fragment[0] * SYNC,), (SYNC,))
    shaped = stepped.reshape(rows, KVH, HD)
    fragment = jnp.take(shaped, heads, axis=1).reshape(rows, SYNC * HD)
    islands = lax.axis_size("island")
    total = lax.psum_scatter(
        fragment.astype(jnp.bfloat16), "island", scatter_dimension=0, tiled=True
    ).astype(jnp.float32)
    base_next, momentum_next = outer_update(base, outer_momentum, total, islands)
    whole_base = lax.all_gather(
        base_next.astype(jnp.bfloat16), "island", axis=0, tiled=True
    ).astype(base_next.dtype)
    updated = shaped.at[:, heads, :].set(whole_base.reshape(rows, SYNC, HD)).reshape(rows, width)
    return (
        updated[None],
        moment_one.astype(jnp.bfloat16)[None],
        moment_two.astype(jnp.bfloat16)[None],
        base_next,
        momentum_next,
    )


def fits(tokens, params, islands, peers):
    span = params.shape[1] // islands
    return (
        peers == 4
        and islands >= 4
        and islands & (islands - 1) == 0
        and span % (2 * HD) == 0
        and tokens.shape[1] % HD == 0
    )


def shards(tokens, cotangent, params, *rest):
    sizes = lax.axis_size("island"), lax.axis_size("fsdp")
    step = staged if fits(tokens, params, *sizes) else plain
    return step(tokens, cotangent, params, *rest)


def solution(mesh):
    placed = (
        P("island", "fsdp", None),
        P("island", "fsdp", None),
        P("island", "fsdp", None),
        P("island", "fsdp", None),
        P("island", "fsdp", None),
        P(("fsdp", "island"), None),
        P(("fsdp", "island"), None),
        P(),
        P(),
    )
    return jax.shard_map(
        shards,
        mesh=mesh,
        in_specs=placed,
        out_specs=(
            P("island", "fsdp", None),
            P("island", "fsdp", None),
            P("island", "fsdp", None),
            P(("fsdp", "island"), None),
            P(("fsdp", "island"), None),
        ),
        check_vma=False,
    )
```

```python
import functools

import jax
import jax.numpy as jnp
from jax import lax
from jax.experimental import pallas as pl
from jax.experimental.pallas import tpu as pltpu
from jax.sharding import PartitionSpec as P


KVH = 8
HD = 128
SYNC = 4


def outer_update(base, outer_momentum, total, islands):
    delta = base - total / islands
    momentum = 0.9 * outer_momentum + delta
    return (base - 0.7 * (delta + 0.9 * momentum), momentum)


ANY = pl.BlockSpec(memory_space=pl.ANY)
HBM = pl.BlockSpec(memory_space=pltpu.HBM)


def cost(flops, moved):
    return pl.CostEstimate(flops=flops, bytes_accessed=moved, transcendentals=0)


def head_at(heads_ref, step_ref, position):
    return heads_ref[lax.rem(step_ref[0] * SYNC + position, KVH)]


def column(heads_ref, step_ref, position):
    return pl.ds(pl.multiple_of(head_at(heads_ref, step_ref, position) * HD, HD), HD)


VMEM_GRANT = 67043328 - 68 * 2**18


def call(
    kernel, scalars, args, outs, scratch, estimate, in_specs=None, out_specs=None, aliases=None
):
    return pl.pallas_call(
        kernel,
        grid_spec=pltpu.PrefetchScalarGridSpec(
            num_scalar_prefetch=len(scalars),
            grid=(1,),
            in_specs=in_specs or [ANY] * len(args),
            out_specs=out_specs or [ANY] * len(outs),
            scratch_shapes=scratch,
        ),
        out_shape=outs,
        input_output_aliases=aliases or {},
        cost_estimate=estimate,
        compiler_params=pltpu.CompilerParams(vmem_limit_bytes=VMEM_GRANT),
    )(*scalars, *args)


def turn_tokens(table, tokens, owners, peers, span, lanes, cuts):
    depth = tokens.shape[0]
    first, count = lanes

    def kernel(table_ref, tok_ref, *refs):
        outs = refs[: len(cuts) * peers]
        raw, in_sems, out_sems = refs[len(cuts) * peers : len(cuts) * peers + 3]
        stages = refs[len(cuts) * peers + 3 :]
        sequence = [*range(1, peers), 0]

        def load(e, i):
            start = (table_ref[owners + e] * owners + i) * span + first
            return pltpu.make_async_copy(
                tok_ref.at[:, pl.ds(pl.multiple_of(start, HD), count)],
                raw.at[e, i],
                in_sems.at[e, i],
            )

        for e in sequence:
            for i in range(owners):
                load(e, i).start()
        stores = []
        for e in sequence:
            for i in range(owners):
                load(e, i).wait()
                turned = raw[e, i].T
                for c, (start, width) in enumerate(cuts):
                    stages[c][e, i] = turned[start - first : start - first + width]
            for c in range(len(cuts)):
                stores.append(
                    pltpu.make_async_copy(
                        stages[c].at[e], outs[c * peers + e], out_sems.at[c, e]
                    )
                )
                stores[-1].start()
        for store in stores:
            store.wait()

    flat = call(
        kernel,
        (table,),
        (tokens,),
        [
            jax.ShapeDtypeStruct((owners, w, depth), tokens.dtype)
            for _, w in cuts
            for _ in range(peers)
        ],
        [
            pltpu.VMEM((peers, owners, depth, count), tokens.dtype),
            pltpu.SemaphoreType.DMA((peers, owners)),
            pltpu.SemaphoreType.DMA((len(cuts), peers)),
            *[pltpu.VMEM((peers, owners, w, depth), tokens.dtype) for _, w in cuts],
        ],
        cost(0, 4 * peers * owners * count * depth),
        in_specs=[HBM],
    )
    return [flat[c * peers : (c + 1) * peers] for c in range(len(cuts))]


def inner_step(heads, step, table, toks, cots, state, olds, place, k0):
    owners, _, _ = state[0].shape
    w, depth = toks[0].shape[1:]
    peers = len(toks)
    p0, count = place
    rows = owners * w
    shared = max(0, min(SYNC - p0, count))

    def kernel(heads_ref, step_ref, table_ref, *refs):
        tok_refs, refs = refs[:peers], refs[peers:]
        cot_refs, refs = refs[: len(cots)], refs[len(cots) :]
        sources, refs = refs[:3], refs[3:]
        if olds is not None:
            refs = refs[3:]
        targets, refs = refs[:3], refs[3:]
        if shared:
            keep_ref, send_ref, *refs = refs
        left, right, grad, p_s, m_s, v_s, tok_sems, cot_sems, in_sems, out_sems = refs
        parts = (p_s, m_s, v_s)
        me = table_ref[owners]
        isle = table_ref[0]
        inner = (me > 0) & (me < peers - 1)

        def tok_copy(e):
            return pltpu.make_async_copy(
                tok_refs[e], left.at[:, :, pl.ds(e * depth, depth)], tok_sems.at[e]
            )

        def cot_copy(e, k, j):
            return pltpu.make_async_copy(
                cot_refs[k].at[:, column(heads_ref, step_ref, p0 + j)],
                right.at[pl.ds(e * depth, depth), pl.ds(j * HD, HD)],
                cot_sems.at[e, j],
            )

        def window(ref, j):
            return ref.at[:, pl.ds(k0, w), column(heads_ref, step_ref, p0 + j)]

        def in_copy(n, j):
            return pltpu.make_async_copy(window(sources[n], j), parts[n].at[j], in_sems.at[n, j])

        def out_copy(n, j):
            return pltpu.make_async_copy(parts[n].at[j], window(targets[n], j), out_sems.at[n, j])

        for e in range(peers):
            tok_copy(e).start()
        for j in range(count):
            for e in range(2):
                cot_copy(e, e, j).start()
        for e in range(2, peers):

            @pl.when(inner)
            def _():
                for j in range(count):
                    cot_copy(e, 2 * e - 2, j).start()

            @pl.when(jnp.logical_not(inner))
            def _():
                for j in range(count):
                    cot_copy(e, 2 * e - 1, j).start()

        for j in range(count):
            for n in range(3):
                in_copy(n, j).start()
        for e in range(peers):
            tok_copy(e).wait()
            for j in range(count):
                cot_copy(e, e, j).wait()

        def update(j, lane, owner, target, slot):
            g = grad[owner, :, lane * HD : (lane + 1) * HD]
            one = 0.9 * m_s[j, owner].astype(jnp.float32) + 0.1 * g
            two = 0.95 * v_s[j, owner].astype(jnp.float32) + 0.05 * g * g
            old = p_s[j, owner]
            new = old - 0.01 * (one / (jnp.sqrt(two) + 1e-08) + 0.1 * old)
            m_s[j, owner] = one.astype(m_s.dtype)
            v_s[j, owner] = two.astype(v_s.dtype)
            p_s[j, owner] = new
            if target is not None:
                lanes = pl.ds(pl.multiple_of(j * HD, HD), HD)
                target[slot, :, lanes] = new.astype(target.dtype)

        def one_pair(share, pair, carry):
            lanes = pl.ds(pl.multiple_of(pair * 2 * HD, 2 * HD), 2 * HD)
            grad[...] = jnp.dot(
                left[...].reshape(rows, peers * depth),
                right[:, lanes],
                preferred_element_type=jnp.float32,
            ).reshape(owners, w, 2 * HD)
            for lane in range(2):
                j = 2 * pair + lane
                for n in range(3):
                    in_copy(n, j).wait()

                def two_owners(slot, carry):
                    for odd, target in enumerate((keep_ref, send_ref) if share else (None, None)):
                        update(j, lane, (2 * slot + odd) ^ isle, target, slot)
                    return carry

                lax.fori_loop(0, owners // 2, two_owners, 0)
                for n in range(3):
                    out_copy(n, j).start()
            return carry

        if shared:
            lax.fori_loop(0, shared // 2, functools.partial(one_pair, True), 0)
        if shared < count:
            lax.fori_loop(shared // 2, count // 2, functools.partial(one_pair, False), 0)
        for j in range(count):
            for n in range(3):
                out_copy(n, j).wait()

    args = [*toks, *cots, *state]
    aliases = {}
    if olds is not None:
        for i in range(3):
            aliases[3 + len(args) + i] = i
        args += list(olds)
    outs = [jax.ShapeDtypeStruct(a.shape, a.dtype) for a in state]
    out_specs = [HBM] * 3
    if shared:
        piece = (owners // 2, w, shared * HD)
        outs += [jax.ShapeDtypeStruct(piece, jnp.bfloat16)] * 2
        out_specs += [pl.BlockSpec(piece, lambda i, *_: (0, 0, 0))] * 2
    states = [HBM] * (6 if olds is not None else 3)
    result = call(
        kernel,
        (heads, step, table),
        args,
        outs,
        [
            pltpu.VMEM((owners, w, peers * depth), toks[0].dtype),
            pltpu.VMEM((peers * depth, count * HD), cots[0].dtype),
            pltpu.VMEM((owners, w, 2 * HD), jnp.float32),
            *[pltpu.VMEM((count, owners, w, HD), a.dtype) for a in state],
            pltpu.SemaphoreType.DMA((peers,)),
            pltpu.SemaphoreType.DMA((peers, count)),
            pltpu.SemaphoreType.DMA((3, count)),
            pltpu.SemaphoreType.DMA((3, count)),
        ],
        cost(
            2 * rows * depth * peers * count * HD,
            rows * count * HD * 16 + 2 * rows * depth * peers,
        ),
        in_specs=[ANY] * (len(toks) + len(cots)) + states,
        out_specs=out_specs,
        aliases=aliases,
    )
    return result[:3], result[3:]


def place_base(heads, step, table, news, params, starts):
    owners = params.shape[0]
    shapes = [near.shape for near, _ in news]
    count = shapes[0][2] // HD

    def kernel(heads_ref, step_ref, table_ref, *refs):
        pieces, refs = refs[: 2 * len(news)], refs[2 * len(news) + 1 :]
        out_ref, stages, sems = refs[0], refs[1:-1], refs[-1]
        isle = table_ref[0]
        copies = []
        for c, (k0, shape) in enumerate(zip(starts, shapes)):
            for j in range(count):
                for e in range(owners):
                    source = pieces[2 * c + e % 2][e // 2, :, j * HD : (j + 1) * HD]
                    stages[c][j, e ^ isle] = source.astype(jnp.float32)
                target = out_ref.at[:, pl.ds(k0, shape[1]), column(heads_ref, step_ref, j)]
                copies.append(pltpu.make_async_copy(stages[c].at[j], target, sems.at[c, j]))
                copies[-1].start()
        for copy in copies:
            copy.wait()

    (out,) = call(
        kernel,
        (heads, step, table),
        (*[x for pair in news for x in pair], params),
        [jax.ShapeDtypeStruct(params.shape, params.dtype)],
        [
            *[pltpu.VMEM((count, owners, shape[1], HD), jnp.float32) for shape in shapes],
            pltpu.SemaphoreType.DMA((len(news), count)),
        ],
        cost(0, sum(owners * shape[1] * shape[2] * 8 for shape in shapes)),
        in_specs=[
            pl.BlockSpec(shape, lambda i, *_: (0, 0, 0)) for shape in shapes for _ in range(2)
        ]
        + [HBM],
        out_specs=[HBM],
        aliases={3 + 2 * len(news): 0},
    )
    return out


def swap(x, axis, mask):
    return lax.ppermute(x, axis, [(i, i ^ mask) for i in range(lax.axis_size(axis))])


def line_gather(own):
    middle, ends = [(1, 2), (2, 1)], [(1, 0), (2, 3)]
    near = swap(own, "fsdp", 1)
    far = lax.ppermute(own, "fsdp", middle)
    next_far = lax.ppermute(near, "fsdp", middle)
    relay = lax.ppermute(far, "fsdp", ends)
    next_relay = lax.ppermute(next_far, "fsdp", ends)
    return [own, near, next_far, relay, far, next_relay]


def island_trade(keep, give, waiting):
    got = swap(give, "island", 1)
    part = keep.astype(jnp.float32) + got.astype(jnp.float32)
    total, rows = part[0], [waiting]
    ahead = 0 if waiting is None else waiting.shape[0]
    for d in range(1, part.shape[0]):
        piece = part[d].astype(jnp.bfloat16)
        if ahead:
            piece = jnp.concatenate([waiting, piece])
        piece = swap(piece, "island", 2 * d)
        rows.append(piece[:ahead])
        total = total + piece[ahead:].astype(jnp.float32)
    return total, rows


def island_rows(rows):
    near = jnp.stack(rows)
    return near, swap(near, "island", 1)


PLAN = ((0, 9), (9, 4), (13, 3))
PARTS = 16


def staged(
    tokens,
    cotangent,
    params,
    first_moment,
    second_moment,
    base,
    outer_momentum,
    head_order,
    step_fragment,
):
    islands = lax.axis_size("island")
    peers = lax.axis_size("fsdp")
    rows, width = params.shape[1:]
    span = rows // islands
    me = lax.axis_index("fsdp").astype(jnp.int32)
    isle = lax.axis_index("island").astype(jnp.int32)
    slots = jnp.arange(islands + peers, dtype=jnp.int32)
    table = jnp.where(slots < islands, slots ^ isle, (slots - islands) ^ me)
    hs = (head_order, step_fragment)

    cots = line_gather(cotangent[0])
    plan = [(k * span // PARTS, n * span // PARTS) for k, n in PLAN]
    last = len(plan) - 1
    edge = -(-plan[0][1] // HD) * HD
    turned = turn_tokens(table, tokens[0], islands, peers, span, (0, edge), plan[:1])
    edge = plan[1][0] // HD * HD
    turned += turn_tokens(
        table, tokens[0], islands, peers, span, (edge, span - edge), plan[1:]
    )
    toks = [
        [pieces[0]] + [swap(pieces[e], "fsdp", e) for e in range(1, peers)]
        for pieces in turned
    ]

    state = [a[0].reshape(islands, span, width) for a in (params, first_moment, second_moment)]
    olds = waiting = None
    bases, momenta, news = [], [], []

    def run(c, place):
        return inner_step(*hs, table, toks[c], cots, state, olds, place, plan[c][0])

    for c, (k0, w) in enumerate(plan):
        if c < last:
            olds, pieces = run(c, (0, KVH))
        else:
            olds, pieces = run(c, (0, SYNC))
            olds, _ = run(c, (SYNC, KVH - SYNC))
        total, rows_in = island_trade(*pieces, waiting)
        if c:
            news.append(island_rows(rows_in))
        new, mom = outer_update(base[k0 : k0 + w], outer_momentum[k0 : k0 + w], total, islands)
        bases.append(new)
        momenta.append(mom)
        waiting = new.astype(jnp.bfloat16)
    rows_in = [waiting]
    for d in range(1, islands // 2):
        rows_in.append(swap(waiting, "island", 2 * d))
    news.append(island_rows(rows_in))
    starts = [k0 for k0, _ in plan]
    out = place_base(*hs, table, news[:last], olds[0], starts[:last])
    out = place_base(*hs, table, news[last:], out, starts[last:])
    return (
        out.reshape(1, rows, width),
        olds[1].reshape(1, rows, width),
        olds[2].reshape(1, rows, width),
        jnp.concatenate(bases),
        jnp.concatenate(momenta),
    )


def plain(
    tokens,
    cotangent,
    params,
    first_moment,
    second_moment,
    base,
    outer_momentum,
    head_order,
    step_fragment,
):
    local_tokens = tokens[0]
    weights = params[0]
    rows = weights.shape[0]
    width = weights.shape[1]
    block = local_tokens.shape[0]
    columns = lax.all_to_all(tokens, "fsdp", split_axis=2, concat_axis=1, tiled=True)[0]
    piece = lax.all_gather(cotangent, "fsdp", axis=1, tiled=True)
    blocks = piece.shape[1] // block

    def one_block(index, running):
        grads_part = lax.dynamic_slice_in_dim(piece[0], index * block, block, 0)
        token_part = lax.dynamic_slice_in_dim(columns, index * block, block, 0)
        part = lax.dot_general(
            token_part, grads_part, (((0,), (0,)), ((), ())), preferred_element_type=jnp.float32
        )
        part = lax.optimization_barrier(part.astype(jnp.bfloat16)).astype(jnp.float32)
        return running + part

    grad = lax.fori_loop(0, blocks, one_block, jnp.zeros((rows, width), jnp.float32))
    moment_one = 0.9 * first_moment[0].astype(jnp.float32) + 0.1 * grad
    moment_two = 0.95 * second_moment[0].astype(jnp.float32) + 0.05 * grad * grad
    stepped = weights - 0.01 * (moment_one / (jnp.sqrt(moment_two) + 1e-08) + 0.1 * weights)
    heads = lax.dynamic_slice(head_order, (step_fragment[0] * SYNC,), (SYNC,))
    shaped = stepped.reshape(rows, KVH, HD)
    fragment = jnp.take(shaped, heads, axis=1).reshape(rows, SYNC * HD)
    islands = lax.axis_size("island")
    total = lax.psum_scatter(
        fragment.astype(jnp.bfloat16), "island", scatter_dimension=0, tiled=True
    ).astype(jnp.float32)
    base_next, momentum_next = outer_update(base, outer_momentum, total, islands)
    whole_base = lax.all_gather(
        base_next.astype(jnp.bfloat16), "island", axis=0, tiled=True
    ).astype(base_next.dtype)
    updated = shaped.at[:, heads, :].set(whole_base.reshape(rows, SYNC, HD)).reshape(rows, width)
    return (
        updated[None],
        moment_one.astype(jnp.bfloat16)[None],
        moment_two.astype(jnp.bfloat16)[None],
        base_next,
        momentum_next,
    )


def fits(tokens, params, islands, peers):
    span = params.shape[1] // islands
    return (
        peers == 4
        and islands >= 4
        and islands & (islands - 1) == 0
        and span % (2 * HD) == 0
        and tokens.shape[1] % HD == 0
    )


def shards(tokens, cotangent, params, *rest):
    sizes = lax.axis_size("island"), lax.axis_size("fsdp")
    step = staged if fits(tokens, params, *sizes) else plain
    return step(tokens, cotangent, params, *rest)


def solution(mesh):
    placed = (
        P("island", "fsdp", None),
        P("island", "fsdp", None),
        P("island", "fsdp", None),
        P("island", "fsdp", None),
        P("island", "fsdp", None),
        P(("fsdp", "island"), None),
        P(("fsdp", "island"), None),
        P(),
        P(),
    )
    return jax.shard_map(
        shards,
        mesh=mesh,
        in_specs=placed,
        out_specs=(
            P("island", "fsdp", None),
            P("island", "fsdp", None),
            P("island", "fsdp", None),
            P(("fsdp", "island"), None),
            P(("fsdp", "island"), None),
        ),
        check_vma=False,
    )
```
